32 devices in a mesh: groups: 2 (over y), tmpl: 4 (over z), chan: 2 (over x), tm: 2 (over core).
Axes of the slice: x: 2, y: 2, z: 4, core: 2. Of those that a mesh axis runs over, the one named last changes fastest.
Arguments:
- samples: bfloat16 [1792, 3584], P(('tmpl', 'chan'), ('groups', 'tm')), parts along dimension 1, may hold values from -6 to 6
- tail: bfloat16 [1792, 1792], P(('tmpl', 'chan'), 'groups'), parts along dimension 1, may hold values from -6 to 6
- templates: bfloat16 [128, 8, 640], P('tmpl', 'chan'), may hold values from -6 to 6
- channels: int32 [128, 8], P('tmpl', 'chan'), may hold values from 0 to 1791
- moveouts: int32 [128, 8], P('tmpl', 'chan'), may hold values from 0 to 256
- live: int32 [128], P('tmpl'), may hold values from 4 to 8
Outputs:
- detection: float32 [128, 3584], P(('tmpl', 'chan'), ('groups', 'tm')), parts along dimension 1
The draws below stay inside these ranges and needn't reach their ends.
There are 2 independent parts, one for each index of `groups`. The reference program is written for one: setup_inputs(seed, part) draws one part's arguments, and reference() takes and returns one part's arrays. A program takes and returns all parts, laid end to end along the dimension named above; an argument that names none is the same for every part. Nothing has to cross between parts.
All inputs are finite; a program needn't handle non-finite values.
Results may differ from the reference program's by a relative error of at most 0.0003.
Values may be sent and summed in bfloat16 or wider, within the bound.
No kernel may reach another device: no remote copies, remote signals or barrier semaphores. Data moves between devices by JAX's collectives and lax.ppermute only.
A program may use at most 64 MiB of HBM per device.

```python
import jax
import jax.numpy as jnp
from jax import lax

CH = 1792
L = 640
MAXS = 256
K = 8
NT = 128
TIME = 1792
HALO = 896


def place_ends(drawn, key, low, top_value):
    index_at = [jax.random.randint(jax.random.fold_in(key, axis), (), 0, length) for axis, length in enumerate(drawn.shape)]
    widest = drawn.shape.index(max(drawn.shape))
    next_to = index_at[:widest] + [(index_at[widest] + 1) % drawn.shape[widest]] + index_at[widest + 1:]
    return drawn.at[tuple(index_at)].set(low).at[tuple(next_to)].set(top_value)


def block_levels(stream_key, extent, shards, low, largest):
    loudness, own = 1.0, jax.random.fold_in(stream_key, 6)
    for axis_at, parts in shards:
        heights = jnp.exp(jax.random.uniform(jax.random.fold_in(own, axis_at), (parts,), jnp.float32, low / len(shards), largest / len(shards)))
        loudness = loudness * jnp.repeat(heights, extent[axis_at] // parts).reshape([-1 if axis == axis_at else 1 for axis in range(len(extent))])
    return loudness


def centred(rng, extent, deviation, limit, shards=(), kind=jnp.bfloat16):
    entries = jax.random.normal(rng, extent, jnp.float32) * deviation
    if len(shards) > 0:
        entries = block_levels(rng, extent, shards, -0.22, 0.18) * entries
    return jnp.clip(entries, min=-limit, max=limit).astype(kind)


def setup_inputs(seed: int = 0, part: int = 0) -> dict:
    splits = jax.random.split(jax.random.key(seed), 7)
    part_splits = jax.random.split(jax.random.fold_in(splits[6], part), 7)
    samples = centred(part_splits[0], (CH, TIME), 1.0, 6.0, ((0, 8), (1, 2)))
    tail = centred(part_splits[1], (CH, HALO), 1.0, 6.0, ((0, 8),))
    templates = centred(splits[2], (NT, K, L), 1.0, 6.0, ((0, 4), (1, 2)))
    channels = place_ends(jax.random.randint(splits[3], (NT, K), 0, CH), jax.random.fold_in(splits[3], 1), 0, CH - 1).astype(jnp.int32)
    moveouts = place_ends(jax.random.randint(splits[4], (NT, K), 0, MAXS + 1), jax.random.fold_in(splits[4], 1), 0, MAXS).astype(jnp.int32)
    live = place_ends(jax.random.randint(splits[5], (NT,), K // 2, K + 1), jax.random.fold_in(splits[5], 1), K // 2, K).astype(jnp.int32)
    return {"samples": samples, "tail": tail, "templates": templates, "channels": channels, "moveouts": moveouts, "live": live}


EPS = 1e-06

def depthwise(signal, kernel, precision):
    output = lax.conv_general_dilated(signal[None], kernel[:, None, :], (1,), 'VALID', dimension_numbers=('NCH', 'OIH', 'NCH'), feature_group_count=signal.shape[0], precision=precision, preferred_element_type=jnp.float32)
    return output[0]

def shifted_rows(window, chan_ids, offsets, length):
    picked = jnp.take(window, chan_ids, axis=0)

    def one_row(row_data, offset):
        return lax.dynamic_slice_in_dim(row_data, offset.astype(jnp.int32), length)
    return jax.vmap(one_row)(picked, offsets)

def reference(samples, tail, templates, channels, moveouts, live):
    window = jnp.concatenate([samples, tail], axis=1)

    def one_template(packed):
        waveform, chan_ids, offsets, used = packed
        slot_data = shifted_rows(window, chan_ids, offsets, TIME + L)
        correlation = depthwise(slot_data, waveform, None)[:, :TIME]
        squares = slot_data.astype(jnp.float32) ** 2
        energy = depthwise(squares, jnp.ones((K, L), jnp.float32), lax.Precision.HIGHEST)[:, :TIME]
        tnorm = jnp.sqrt(lax.optimization_barrier(jnp.sum(waveform.astype(jnp.float32) ** 2, axis=-1)) + EPS)
        ncc = correlation / (tnorm[:, None] * jnp.sqrt(energy + EPS))
        used_f = used.astype(jnp.float32)
        weight = jnp.where(jnp.arange(K) < used, jnp.sqrt(jnp.float32(L) / used_f), jnp.float32(0.0))
        return lax.optimization_barrier(jnp.sum(weight[:, None] * ncc, axis=0))
    return lax.map(one_template, (templates, channels, moveouts, live))
```

```python
import jax
import jax.numpy as jnp
from jax import lax
from jax.experimental import pallas as pl
from jax.experimental.pallas import tpu as pltpu
from jax.sharding import PartitionSpec as P


EPS = 1e-06
LANES = 128
DEPTH = 16
BATCH = 16
F32 = jnp.float32
BF16 = jnp.bfloat16
GROUP = ("tmpl", "chan")


def bucket_rows(slots, buckets):
    mean = slots / buckets
    return 16 * int(-(-(mean + 4 * mean**0.5) // 16))


def spot_of(i):
    return LANES // DEPTH - 1 - i % (LANES // DEPTH)


def iota(shape, axis):
    return lax.broadcasted_iota(jnp.int32, shape, axis)


def across(a, b):
    return lax.dot_general(a, b, (((1,), (1,)), ((), ())), preferred_element_type=F32)


def here():
    return lax.axis_index("tmpl") * lax.axis_size("chan") + lax.axis_index("chan")


def pack_kernel(groups, depth, owned, turn, templates_in, channels_in, moveouts_in, live_in, *rest):
    outs = rest[: len(groups)]
    templates, channels, moveouts, live, lined, sems = rest[len(groups) :]
    copies = [
        pltpu.make_async_copy(a, b, sems.at[i])
        for i, (a, b) in enumerate(
            ((channels_in, channels), (moveouts_in, moveouts), (live_in, live), (templates_in, templates))
        )
    ]
    for copy in copies:
        copy.start()
    first = F32(0) if turn is None else (turn[0] * depth).astype(F32)
    per_slot, rows = channels.shape
    slots, length = lined.shape
    for copy in copies[:3]:
        copy.wait()
    used = jnp.broadcast_to(live[...], (per_slot, rows))
    position = iota((per_slot, rows), 0) + lax.axis_index("chan") * per_slot
    owner = channels[...] // owned
    tag = jnp.where(position < used, owner, -1)
    widen = jnp.where(iota((rows, slots), 1) // per_slot == iota((rows, slots), 0), 1.0, 0.0).astype(BF16)
    own_row = iota((per_slot, slots), 1) % per_slot == iota((per_slot, slots), 0)

    def line(values):
        wide = jnp.dot(values.astype(F32).astype(BF16), widen, preferred_element_type=F32)
        return jnp.sum(jnp.where(own_row, wide, 0.0), axis=0, keepdims=True)

    tag_line = line(tag)
    tag_row = jnp.broadcast_to(tag_line, (slots, slots))
    same = (tag_row.T == tag_row) & (iota((slots, slots), 0) < iota((slots, slots), 1))
    rank = jnp.sum(jnp.where(same, 1.0, 0.0), axis=0, keepdims=True)
    rounds = jnp.ceil((jnp.max(jnp.where(tag_line >= 0, rank, -1.0)) + 1.0) / depth)
    known = [channels[...] - owner * owned, moveouts[...], iota((per_slot, rows), 1), used]
    facts = jnp.zeros((LANES, slots), F32)
    which = iota((LANES, slots), 0)
    for at, fact in enumerate(known):
        facts = jnp.where(which == at, jnp.broadcast_to(line(fact), (LANES, slots)), facts)
    facts = facts.astype(BF16)
    copies[3].wait()
    for n in range(rows):
        lined[per_slot * n : per_slot * (n + 1), :] = templates[n].astype(F32)
    flip_row, flip_lane = iota((LANES, LANES), 0), iota((LANES, LANES), 1)
    mirrored = flip_row // DEPTH * DEPTH + DEPTH - 1 - flip_row % DEPTH
    flip = jnp.where(flip_lane == mirrored, 1.0, 0.0).astype(BF16)
    tiles = [
        jnp.dot(lined[:, LANES * q : LANES * (q + 1)].astype(BF16), flip, preferred_element_type=F32).astype(BF16)
        for q in range(length // LANES)
    ]
    place = lax.axis_index("tmpl").astype(F32)
    for out, owners in zip(outs, groups, strict=True):
        blocks, told = [], []
        for to in owners:
            fits = (tag_line == to.astype(F32)) & (tag_line >= 0) & (rank - first == iota((depth, slots), 0).astype(F32))
            block = jnp.where(fits, 1.0, 0.0)
            count = jnp.sum(block)
            lane = iota((depth, LANES), 1)
            extra = jnp.where(lane == 4, count, jnp.where(lane == 5, rounds, jnp.where(lane == 6, place, 0.0)))
            blocks.append(block.astype(BF16))
            told.append(across(block.astype(BF16), facts) + extra)
        chosen = jnp.concatenate(blocks, axis=0)
        for q, tile in enumerate(tiles):
            out[:, LANES * q : LANES * (q + 1)] = jnp.dot(chosen, tile, preferred_element_type=F32).astype(BF16)
        out[:, length:] = jnp.concatenate(told, axis=0).astype(BF16)


def pack(turn, templates, channels, moveouts, live, sizes, targets, depth, owned):
    rows, per_slot, length = templates.shape
    slots = rows * per_slot

    def kernel(*refs):
        turns, refs = (refs[0], refs[1:]) if turn is not None else (None, refs)
        pack_kernel(targets(), depth, owned, turns, *refs)

    smem = [] if turn is None else [pl.BlockSpec(memory_space=pltpu.SMEM)]
    args = (templates, channels.T, moveouts.T, live[None, :])
    return pl.pallas_call(
        kernel,
        out_shape=[jax.ShapeDtypeStruct((size * depth, length + LANES), BF16) for size in sizes],
        in_specs=smem + [pl.BlockSpec(memory_space=pl.ANY)] * 4,
        out_specs=[pl.BlockSpec(memory_space=pltpu.VMEM)] * len(sizes),
        scratch_shapes=[pltpu.VMEM(a.shape, a.dtype) for a in args]
        + [pltpu.VMEM((slots, length), F32), pltpu.SemaphoreType.DMA((4,))],
        compiler_params=pltpu.CompilerParams(vmem_limit_bytes=8 << 20),
        name="pack",
    )(*(() if turn is None else (turn.reshape(1),)), *args)


def match_kernel(dims, n_parcels, n_outs, *refs):
    near, after, tail = refs[:3]
    parcels = refs[3 : 3 + n_parcels]
    outs = refs[3 + n_parcels : 3 + n_parcels + n_outs]
    rounds_out, *refs = refs[3 + n_parcels + n_outs :]
    window, waves, scores, named, squares, sums, facts_v, facts, order, sem, hankel, toeplitz, group = refs
    depth, per_dev, per_owner, length, block = dims
    tiles, wave_tiles = block // LANES, length // LANES
    spread = tiles + wave_tiles
    owned = near.shape[0]
    rows = waves.shape[1]
    names = sum(out.shape[0] for out in outs)
    is_last = lax.axis_index("tm") == lax.axis_size("tm") - 1
    me = here() if n_outs > 1 else 0

    def line_of(place, n):
        name = place * per_dev + n
        return ((name // per_owner) ^ me) * per_owner + name % per_owner

    pick_fact = jnp.where(iota((8, LANES), 0) == iota((8, LANES), 1), 1.0, 0.0).astype(BF16)
    begin = 0
    for parcel in parcels:
        size = parcel.shape[0]
        known = across(pick_fact, parcel[:, length:]).astype(jnp.int32)
        shift = known[1:2, :]
        facts_v[0:1, begin : begin + size] = (shift // LANES * owned + known[0:1, :]) * LANES + shift % LANES
        facts_v[1:3, begin : begin + size] = known[4:6, :]
        begin += size
    tell = pltpu.make_async_copy(facts_v, facts, sem)
    tell.start()

    begin = 0
    for parcel in parcels:
        size = parcel.shape[0]
        for t in range(wave_tiles + 1):
            waves[t, begin : begin + size, :] = parcel[:, LANES * t : LANES * (t + 1)].astype(F32)
        begin += size
    for t in range(tiles):
        window[owned * t : owned * (t + 1), :] = near[:, LANES * t : LANES * (t + 1)].astype(F32)

    @pl.when(is_last)
    def _():
        for t in range(tiles):
            window[owned * (tiles + t) : owned * (tiles + t + 1), :] = tail[:, LANES * t : LANES * (t + 1)].astype(F32)

    @pl.when(jnp.logical_not(is_last))
    def _():
        for t in range(tiles):
            window[owned * (tiles + t) : owned * (tiles + t + 1), :] = after[:, LANES * t : LANES * (t + 1)].astype(F32)

    filled = 2 * tiles * owned
    if filled < window.shape[0]:
        window[filled:, :] = jnp.zeros((window.shape[0] - filled, LANES), F32)
    toeplitz[...] = jnp.zeros(toeplitz.shape, BF16)
    row, lane = iota(sums.shape, 0) % LANES, iota(sums.shape, 1)
    place, part = lane % LANES, lane // LANES
    keep = jnp.where(part == 0, row - place, jnp.where(part == 1, 0, place - row - 1))
    sums[...] = jnp.where(keep >= 0, 1.0, 0.0).astype(BF16)
    tell.wait()

    def list_block(b, carry):
        total, most = carry
        count = facts[1, b * depth]

        def put(eight, _):
            for i in range(8):
                at = b * depth + 8 * eight + i
                order[0, total + 8 * eight + i] = at
                order[1, total + 8 * eight + i] = facts[0, at]
            return 0

        lax.fori_loop(0, (count + 7) // 8, put, 0)
        return total + count, jnp.maximum(most, facts[2, b * depth])

    total, most = lax.fori_loop(0, rows // depth, list_block, (jnp.int32(0), jnp.int32(0)))
    rounds_out[0] = most

    per_tile = LANES // DEPTH
    lane8, sub8 = iota((8, LANES), 1), iota((8, LANES), 0)
    pick_row, pick_lane = iota((BATCH, BATCH * DEPTH), 0), iota((BATCH, BATCH * DEPTH), 1)
    pick_start = pick_row // per_tile * LANES + spot_of(pick_row) * DEPTH
    pick = jnp.where(pick_lane == pick_start + DEPTH - 1, 1.0, 0.0).astype(BF16)

    def build(step):
        last = [jnp.minimum(step * BATCH + i, total - 1) for i in range(BATCH)]
        at = [order[0, i] for i in last]
        word = [order[1, i] for i in last]
        for i in range(BATCH):
            for t in range(wave_tiles + 1):
                group[i : i + 1, LANES * t : LANES * (t + 1)] = waves[t, pl.ds(at[i], 1), :]
        for i in range(BATCH):
            within = lax.bitwise_and(word[i], LANES - 1)
            source = lax.shift_right_logical(word[i], LANES.bit_length() - 1)
            turned = [
                pltpu.roll(window[pl.ds(source + owned * t, 8, stride=0), :], LANES - within, 1)
                for t in range(spread + 2)
            ]
            ahead = lane8 + within < LANES
            aligned = [jnp.where(ahead, turned[t], turned[t + 1]) for t in range(spread + 1)]
            halves = []
            for half in range(DEPTH // 8):
                behind = DEPTH - 1 - 8 * half
                rolled = [pltpu.roll(line, LANES - behind, 1, stride=1, stride_axis=0) for line in aligned]
                inside = lane8 + behind - sub8 < LANES
                halves.append([jnp.where(inside, rolled[t], rolled[t + 1]) for t in range(spread)])
            line0 = LANES * (i // per_tile) + DEPTH * spot_of(i)
            for t in range(spread):
                both = jnp.concatenate([h[t] for h in halves], axis=0).astype(BF16)
                hankel[line0 : line0 + DEPTH, LANES * t : LANES * (t + 1)] = both
        for pair in range(BATCH // 2):
            block_tile = 2 * pair // per_tile
            for q in range(wave_tiles):
                two = []
                for i in (2 * pair, 2 * pair + 1):
                    line = waves[q, pl.ds(at[i], 8, stride=0), :]
                    turned = pltpu.roll(line, 0, 1, stride=DEPTH, stride_axis=0)
                    two.append(jnp.where(lane8 // DEPTH == spot_of(i), turned, 0.0))
                toeplitz[
                    q * BATCH * 8 + 16 * pair : q * BATCH * 8 + 16 * pair + 16,
                    LANES * block_tile : LANES * (block_tile + 1),
                ] = jnp.concatenate(two, axis=0).astype(BF16)

    def folded(stack, gap):
        odd = (sub8 // gap) % 2 == 1
        merged = []
        for a, b in zip(stack[: len(stack) // 2], stack[len(stack) // 2 :], strict=True):
            other = jnp.where(odd, a, b)
            back = pltpu.roll(other, gap, 0)
            if gap != 4:
                back = jnp.where(odd, back, pltpu.roll(other, 8 - gap, 0))
            merged.append(jnp.where(odd, b, a) + back)
        return merged

    def solve(step):
        wide = (tiles + 1) * LANES
        parts = jnp.zeros((BATCH * 8, wide), F32)
        for q in range(wave_tiles):
            parts = parts + jnp.dot(
                toeplitz[q * BATCH * 8 : (q + 1) * BATCH * 8, :],
                hankel[:, LANES * q : LANES * q + wide],
                preferred_element_type=F32,
            )
        plain = jnp.dot(pick, hankel[...], preferred_element_type=F32)
        square = plain * plain
        high = square.astype(BF16)
        low = (square - high.astype(F32)).astype(BF16)
        for t in range(spread):
            squares[BATCH * t : BATCH * (t + 1), :LANES] = high[:, LANES * t : LANES * (t + 1)]
            squares[BATCH * t : BATCH * (t + 1), LANES:] = low[:, LANES * t : LANES * (t + 1)]
        swept = jnp.dot(squares[...], sums[...], preferred_element_type=F32)

        def of_tile(t, which):
            return swept[BATCH * t : BATCH * (t + 1), LANES * which : LANES * (which + 1)]

        held = group[...]
        wave = held[:, :length]
        strength = jnp.sum(wave * wave, axis=1, keepdims=True)
        used = held[:, length + 3 : length + 4]
        valid = iota((BATCH, 1), 0) + step * BATCH < total
        spot = line_of(held[:, length + 6 : length + 7].astype(jnp.int32), held[:, length + 2 : length + 3].astype(jnp.int32))
        begin = pl.multiple_of(step * BATCH, BATCH)
        named[pl.ds(begin, BATCH), :] = jnp.where(iota((BATCH, names), 1) == spot, 1.0, 0.0)
        scale = jnp.where(valid, jnp.sqrt(length / used) / jnp.sqrt(strength + EPS), 0.0)

        sheared = []
        for i in range(BATCH):
            piece = (spot_of(i) + 8 - sub8) % 8
            own = [parts[8 * i : 8 * i + 8, LANES * t : LANES * (t + 1)] for t in range(tiles + 1)]
            stay = lane8 >= DEPTH * piece
            sheared.append(
                [
                    pltpu.roll(jnp.where(stay, own[t], own[t + 1]), 0, 1, stride=DEPTH, stride_axis=0)
                    for t in range(tiles)
                ]
            )
        for t in range(tiles):
            energy = of_tile(t, 0) + of_tile(t + wave_tiles, 2)
            for q in range(1, wave_tiles):
                energy = energy + of_tile(t + q, 1)
            weight = scale * lax.rsqrt(energy + EPS)
            for g in range(BATCH // 8):
                stack = [sheared[8 * g + i][t] for i in range(8)]
                for gap in (4, 2, 1):
                    stack = folded(stack, gap)
                straight = pltpu.roll(stack[0], DEPTH, 1, stride=DEPTH, stride_axis=0)
                result = straight * weight[8 * g : 8 * g + 8, :]
                scores[pl.ds(begin + 8 * g, 8), LANES * t : LANES * (t + 1)] = result

    def one_step(step, _):
        build(step)
        solve(step)
        return 0

    lax.fori_loop(0, (total + BATCH - 1) // BATCH, one_step, 0)
    for out in outs:
        out[...] = jnp.zeros(out.shape, F32)

    def stack_up(chunk, _):
        begin = pl.multiple_of(chunk * LANES, LANES)
        there = iota((LANES, 1), 0) + begin < total
        value = jnp.where(there, scores[pl.ds(begin, LANES), :], 0.0)
        where_to = jnp.where(there, named[pl.ds(begin, LANES), :], 0.0).astype(BF16)
        whole = jnp.zeros((names, block), F32)
        for _ in range(3):
            piece = value.astype(BF16)
            value = value - piece.astype(F32)
            whole = whole + lax.dot_general(where_to, piece, (((0,), (0,)), ((), ())), preferred_element_type=F32)
        begin = 0
        for out in outs:
            out[...] += whole[begin : begin + out.shape[0], :]
            begin += out.shape[0]
        return 0

    lax.fori_loop(0, (total + LANES - 1) // LANES, stack_up, 0)


def match(near, after, tail, parcels, sizes, dims):
    length, block = dims[-2:]
    tiles, wave_tiles = block // LANES, length // LANES
    spread = tiles + wave_tiles
    reach = (tail.shape[1] - length) // LANES
    rows = sum(parcel.shape[0] for parcel in parcels)
    wide = -(-rows // LANES) * LANES
    vmem = pl.BlockSpec(memory_space=pltpu.VMEM)
    *parts, rounds = pl.pallas_call(
        lambda *refs: match_kernel(dims, len(parcels), len(sizes), *refs),
        out_shape=[jax.ShapeDtypeStruct((size, block), F32) for size in sizes]
        + [jax.ShapeDtypeStruct((1,), jnp.int32)],
        in_specs=[vmem] * (3 + len(parcels)),
        out_specs=[vmem] * len(sizes) + [pl.BlockSpec(memory_space=pltpu.SMEM)],
        scratch_shapes=[
            pltpu.VMEM((max(2 * tiles, spread + 2 + reach) * near.shape[0], LANES), F32),
            pltpu.VMEM((wave_tiles + 1, rows, LANES), F32),
            pltpu.VMEM((wide, block), F32),
            pltpu.VMEM((wide, sum(sizes)), F32),
            pltpu.VMEM((BATCH * spread, 2 * LANES), BF16),
            pltpu.VMEM((2 * LANES, 3 * LANES), BF16),
            pltpu.VMEM((8, wide), jnp.int32),
            pltpu.SMEM((8, wide), jnp.int32),
            pltpu.SMEM((2, wide + LANES), jnp.int32),
            pltpu.SemaphoreType.DMA,
            pltpu.VMEM((BATCH * DEPTH, spread * LANES), BF16),
            pltpu.VMEM((wave_tiles * BATCH * 8, BATCH * DEPTH), BF16),
            pltpu.VMEM((BATCH, length + LANES), F32),
        ],
        compiler_params=pltpu.CompilerParams(vmem_limit_bytes=24 << 20),
        name="match",
    )(near, after, tail, *parcels)
    return parts, rounds


def serves_directly(buckets, cores):
    return buckets == 8 and cores == 2


def other_core(x):
    return lax.ppermute(x, "tm", [(0, 1), (1, 0)])


def body(samples, tail, templates, channels, moveouts, live):
    block = samples.shape[1]
    per_dev, per_slot, length = templates.shape
    slots = per_dev * per_slot
    buckets = lax.axis_size("tmpl") * lax.axis_size("chan")
    names = lax.axis_size("tmpl") * per_dev
    cores = lax.axis_size("tm")
    depth = bucket_rows(slots, buckets)
    per_owner = names // buckets
    dims = (depth, per_dev, per_owner, length, block)
    after = lax.ppermute(samples, "tm", [(i, i - 1) for i in range(1, cores)])
    direct = serves_directly(buckets, cores)
    routes = ((7, 6), (4, 5), (2, 3), (1, 0))

    def targets():
        if not direct:
            return [[jnp.int32(b) for b in range(buckets)]]
        me, core = here(), lax.axis_index("tm")
        found = [[me]]
        for first, second in routes:
            differ = jnp.where(core == 0, first, second)
            found.append([jnp.where(differ == 0, -2, me ^ differ)])
        return found

    def one_round(turn):
        sizes = [1] * (1 + len(routes)) if direct else [buckets]
        parcels = pack(turn, templates, channels, moveouts, live, sizes, targets, depth, samples.shape[0])
        if direct:
            got = []
            for parcel, differs in zip(parcels[1:], routes, strict=True):
                pairs = [
                    (c * cores + t, (c ^ differ) * cores + t)
                    for c in range(buckets)
                    for t, differ in enumerate(differs)
                    if differ
                ]
                got.append(lax.ppermute(parcel, GROUP + ("tm",), pairs))
            parcels = [parcels[0], *got, *[other_core(g) for g in got]]
        else:
            parcels = [lax.all_to_all(parcels[0], GROUP, 0, 0, tiled=True)]
        outs = [per_owner] * buckets if direct else [names]
        return match(samples, after, tail, parcels, outs, dims)

    parts, rounds = one_round(None)

    def more(state):
        return state[0] < rounds[0]

    def again(state):
        turn, values = state
        return turn + 1, [value + other for value, other in zip(values, one_round(turn)[0], strict=True)]

    _, parts = lax.while_loop(more, again, (jnp.int32(1), parts))
    if not direct:
        spread = lax.all_to_all(parts[0], GROUP, 0, 0, tiled=True)
        return jnp.sum(spread.reshape(buckets, per_owner, block), axis=0)
    result = parts[0]
    for differ in range(buckets - 1, 0, -1):
        other = lax.ppermute(parts[differ], GROUP, [(c, c ^ differ) for c in range(buckets)])
        result = result + other
    return result


def solution(mesh):
    in_specs = (
        P(("tmpl", "chan"), ("groups", "tm")),
        P(("tmpl", "chan"), "groups"),
        P("tmpl", "chan", None),
        P("tmpl", "chan"),
        P("tmpl", "chan"),
        P("tmpl"),
    )
    out_specs = P(("tmpl", "chan"), ("groups", "tm"))
    return jax.shard_map(body, mesh=mesh, in_specs=in_specs, out_specs=out_specs, check_vma=False)
```
